256 devices in a mesh: req: 64 (over z, x, core), tp: 4 (over y).
Axes of the slice: x: 4, y: 4, z: 8, core: 2. Of those that a mesh axis runs over, the one named last changes fastest.
Arguments:
- hidden: bfloat16 [2048, 5120], P('req', 'tp'), may hold values from -8 to 8
- gain: float32 [5120], replicated, may hold values from 0.5 to 1.5
- head_weight: bfloat16 [5120, 131072], P(None, ('req', 'tp')), may hold values from -0.3 to 0.3
- token_ids: int32 [2048], P('req'), may hold values from 0 to 131071
- lengths: int32 [64], P('req'), may hold values from 1 to 32, as said below
- owner_device: int32 [64], replicated, may hold values from 0 to 63, each once
Outputs:
- logprob: float32 [2048], P('req')
- entropy: float32 [2048], P('req')
The draws below stay inside these ranges and needn't reach their ends.
Inputs may be any that keep to these rules, and one draw needn't show every extreme that they name: `lengths`: each sequence has 1 to 32 live slots; some sequence has exactly 32. `owner_device`: A permutation of the req indices.
All inputs are finite; a program needn't handle non-finite values.
Results may differ from the reference program's by a relative error of at most 0.0041.
Values may be sent and summed in bfloat16 or wider, within the bound.
No kernel may reach another device: no remote copies, remote signals or barrier semaphores. Data moves between devices by JAX's collectives and lax.ppermute only.
A program may use at most 128 MiB of HBM per device.

```python
import math
import jax
import jax.numpy as jnp
import numpy as np
from jax import lax

D = 5120
VOCAB = 131072
LEN = 32
TOKENS = 2048
N_REQ = 64


def draw_hidden(key, part):
    values = jnp.clip(jax.random.normal(jax.random.fold_in(key, 5), (TOKENS, D), jnp.float32), -6.0, 6.0)
    return values.astype(jnp.bfloat16)


def draw_head_weight(key, part):
    column_scale = 2.0 * (1.0 + 2.0 * jnp.arange(VOCAB, dtype=jnp.float32) / VOCAB) / jnp.sqrt(jnp.float32(D))
    values = jnp.clip(jax.random.normal(jax.random.fold_in(key, 8), (D, VOCAB), jnp.float32), -3.0, 3.0) * column_scale
    return jnp.clip(values, -7.9, 7.9).astype(jnp.bfloat16)


def draw_lengths(key, part):
    lengths = jax.random.randint(jax.random.fold_in(key, 9), (N_REQ,), 1, LEN + 1)
    longest = jax.random.randint(jax.random.fold_in(key, 10), (), 0, N_REQ)
    return lengths.at[longest].set(LEN).astype(jnp.int32)


def with_ends(result, own_key, low, high):
    shape = result.shape
    place = [jax.random.randint(jax.random.fold_in(own_key, axis), (), 0, shape[axis]) for axis in range(len(shape))]
    result = result.at[tuple(place)].set(low)
    longest = shape.index(max(shape))
    place[longest] = (place[longest] + 1) % shape[longest]
    return result.at[tuple(place)].set(high)


def wide_ids(stream_key, shape, amount, slope):
    weights = [min(1 << octave, amount + 1 - (1 << octave)) * (1 << 20) // math.isqrt((1 << octave) ** slope) + 1 for octave in range((amount + 1).bit_length()) if 1 << octave <= amount]
    spread = 1 + sum(weights) // (1 << 30)
    grid = np.cumsum(np.array([max(1, weight // spread) for weight in weights]))
    ticket = jax.random.randint(jax.random.fold_in(stream_key, 1), shape, 0, int(grid[len(weights) - 1]))
    start = jnp.left_shift(1, jnp.searchsorted(jnp.asarray(grid, jnp.int32), ticket, side="right").astype(jnp.int32))
    standing = start - 1 + jax.random.randint(jax.random.fold_in(stream_key, 4), shape, 0, 1 << 30) % jnp.minimum(start, amount + 1 - start)
    return jax.random.permutation(jax.random.fold_in(stream_key, 2), amount)[standing].astype(jnp.int32)


def setup_inputs(seed: int = 0) -> dict:
    seeds = jax.random.split(jax.random.key(seed), 7)
    hidden = draw_hidden(jax.random.fold_in(seeds[6], 71), 0)
    gain = jnp.clip(1.0 + 0.1 * jax.random.normal(seeds[1], (D,), jnp.float32), 0.5, 1.5)
    head_weight = draw_head_weight(jax.random.fold_in(seeds[6], 71), 0)
    token_ids = with_ends(wide_ids(seeds[3], (TOKENS,), VOCAB, 2), jax.random.fold_in(seeds[3], 3), 0, VOCAB - 1).astype(jnp.int32)
    lengths = draw_lengths(jax.random.fold_in(seeds[6], 71), 0)
    owner_device = jax.random.permutation(seeds[5], N_REQ).astype(jnp.int32)
    return {"hidden": hidden, "gain": gain, "head_weight": head_weight, "token_ids": token_ids, "lengths": lengths, "owner_device": owner_device}


def reference(hidden, gain, head_weight, token_ids, lengths, owner_device):
    values = hidden.astype(jnp.float32)
    mean_square = lax.optimization_barrier(jnp.mean(values * values, axis=-1, keepdims=True))
    normed = (values * lax.rsqrt(mean_square + 1e-05) * gain).astype(jnp.bfloat16)
    row_blocks = normed.reshape(-1, 64, normed.shape[1])
    block_ids = token_ids.reshape(-1, 64)

    def score_block(block_args):
        block_rows, ids_block = block_args
        logits = jnp.dot(block_rows, head_weight, preferred_element_type=jnp.float32)
        peak_logit = lax.optimization_barrier(jnp.max(logits, axis=-1, keepdims=True))
        weights_exp = jnp.exp(logits - peak_logit)
        exp_total = lax.optimization_barrier(jnp.sum(weights_exp, axis=-1))
        exp_spread = lax.optimization_barrier(jnp.sum(weights_exp * logits, axis=-1))
        log_total = peak_logit[:, 0] + jnp.log(exp_total)
        picked = jnp.take_along_axis(logits, ids_block[:, None].astype(jnp.int32), axis=1)[:, 0]
        return (picked - log_total, log_total - exp_spread / exp_total)
    row_logprob, row_entropy = lax.map(score_block, (row_blocks, block_ids))
    row_logprob = row_logprob.reshape(N_REQ, LEN)[owner_device]
    row_entropy = row_entropy.reshape(N_REQ, LEN)[owner_device]
    live_mask = jnp.arange(LEN, dtype=jnp.int32)[None, :] < lengths[:, None]
    logprob = jnp.where(live_mask, row_logprob, jnp.float32(0.0)).reshape(-1)
    entropy = jnp.where(live_mask, row_entropy, jnp.float32(0.0)).reshape(-1)
    return (logprob, entropy)
```

```python
import functools

import jax
import jax.numpy as jnp
from jax import lax
from jax.experimental import pallas as pl
from jax.experimental.pallas import tpu as pltpu
from jax.sharding import Mesh
from jax.sharding import PartitionSpec as P


ALL = ("z", "x", "core", "tp")
SIZES = {"z": 8, "x": 4, "core": 2, "tp": 4}
LANES = 128


def pairs(first, second, sign):
    out = []
    for z in range(8):
        for x in range(4):
            for core, axis in enumerate((first, second)):
                if axis is None:
                    continue
                nz = (z + sign) % 8 if axis == "z" else z
                nx = (x + sign) % 4 if axis == "x" else x
                out.append(((z * 4 + x) * 2 + core, (nz * 4 + nx) * 2 + core))
    return out


def send(value, first, second, sign):
    return lax.ppermute(value, ("z", "x", "core"), pairs(first, second, sign))


def score_kernel(n_parts, width, base_ref, *refs):
    parts, (w_own, w_other, out_ref, logits) = refs[:n_parts], refs[n_parts:]
    rows = parts[0].shape[0]
    cols = w_own.shape[1]
    tile = 256
    for half, w in enumerate((w_own, w_other)):

        def column_tile(n, carry, half=half, w=w):
            at = pl.multiple_of(n * tile, tile)
            lhs = jnp.concatenate([part[:, :width] for part in parts], axis=0)
            product = jnp.dot(lhs, w[:, pl.ds(at, tile)], preferred_element_type=jnp.float32)
            logits[:, pl.ds(pl.multiple_of(half * cols + n * tile, tile), tile)] = product
            return carry

        lax.fori_loop(0, cols // tile, column_tile, 0)

    lane = lax.broadcasted_iota(jnp.int32, (32, LANES), 1)
    slot = lax.broadcasted_iota(jnp.int32, (32, LANES), 0)
    column = lax.broadcasted_iota(jnp.int32, (32, 2 * cols), 1)
    vocab = jnp.where(column < cols, base_ref[0] + column, base_ref[1] + column - cols)
    digit = jnp.where(lane == 0, 4096.0, jnp.where(lane == 1, 64.0, jnp.where(lane == 2, 1.0, 0.0)))
    for i, part in enumerate(parts):

        def group(g, carry, i=i, part=part):
            row = pl.multiple_of(g * 32, 32)
            lg = logits[pl.ds(pl.multiple_of(i * rows + g * 32, 32), 32), :]
            code = part[pl.ds(row, 32), pl.ds(width, LANES)].astype(jnp.float32)
            ids = jnp.sum(code * digit, axis=1, keepdims=True).astype(jnp.int32)
            peak = jnp.max(lg, axis=1, keepdims=True)
            weight = jnp.exp(lg - peak)
            total = jnp.sum(weight, axis=1, keepdims=True)
            spread = jnp.sum(weight * lg, axis=1, keepdims=True)
            pick = jnp.sum(jnp.where(vocab == ids, lg, 0.0), axis=1, keepdims=True)
            stat = jnp.where(lane < 32, peak, jnp.where(lane < 64, total, jnp.where(lane < 96, spread, pick)))
            line = jnp.sum(jnp.where(lane % 32 == slot, stat, 0.0), axis=0, keepdims=True)
            out_ref[pl.ds(i * (rows // 32) + g, 1), :] = line
            return carry

        lax.fori_loop(0, rows // 32, group, 0)


def score(parts, w_own, w_other, bases):
    rows = parts[0].shape[0]
    n = len(parts)
    width = w_own.shape[0]
    cols = w_own.shape[1]
    vmem = pl.BlockSpec(memory_space=pltpu.VMEM)
    return pl.pallas_call(
        functools.partial(score_kernel, n, width),
        out_shape=jax.ShapeDtypeStruct((n * rows // 32, LANES), jnp.float32),
        in_specs=[pl.BlockSpec(memory_space=pltpu.SMEM)] + [vmem] * (n + 2),
        out_specs=vmem,
        scratch_shapes=[pltpu.VMEM((n * rows, 2 * cols), jnp.float32)],
        cost_estimate=pl.CostEstimate(
            flops=4 * n * rows * width * cols, bytes_accessed=n * rows * width * 2, transcendentals=2 * n * rows * cols
        ),
        name="score",
    )(bases, *parts, w_own, w_other)


def table_kernel(place_ref, owner_ref, *refs):
    lines, (out_ref, table) = refs[:-2], refs[-2:]
    table[...] = jnp.zeros_like(table)
    at = 0
    for line in lines:
        for i in range(line.shape[0]):
            table[pl.ds(place_ref[at], 1), :] = line[i : i + 1, :]
            at += 1
    copies = out_ref.shape[0] // table.shape[0]

    def deal(o, carry):
        row = table[pl.ds(owner_ref[o], 1), :]
        for c in range(copies):
            out_ref[pl.ds(o * copies + c, 1), :] = row
        return carry

    lax.fori_loop(0, table.shape[0], deal, 0)


def deal_lines(place, owner, lines, copies):
    smem = pl.BlockSpec(memory_space=pltpu.SMEM)
    vmem = pl.BlockSpec(memory_space=pltpu.VMEM)
    groups = owner.shape[0]
    return pl.pallas_call(
        table_kernel,
        out_shape=jax.ShapeDtypeStruct((groups * copies, LANES), jnp.float32),
        in_specs=[smem, smem] + [vmem] * len(lines),
        out_specs=vmem,
        scratch_shapes=[pltpu.VMEM((groups, LANES), jnp.float32)],
        name="deal",
    )(place, owner, *lines)


def merge_kernel(length_ref, lines_ref, logprob_ref, entropy_ref):
    lines = lines_ref[...]
    total = pltpu.roll(lines, 96, 1)
    spread = pltpu.roll(lines, 64, 1)
    pick = pltpu.roll(lines, 32, 1)
    lane = lax.broadcasted_iota(jnp.int32, lines.shape, 1)
    live = (total > 0.0) & (lane < 32)
    peak = jnp.max(jnp.where(live, lines, -jnp.inf), axis=0, keepdims=True)
    scale = jnp.where(live, jnp.exp(lines - peak), 0.0)
    exp_total = jnp.sum(jnp.where(live, scale * total, 0.0), axis=0, keepdims=True)
    exp_spread = jnp.sum(jnp.where(live, scale * spread, 0.0), axis=0, keepdims=True)
    picked = jnp.sum(jnp.where(live, pick, 0.0), axis=0, keepdims=True)
    log_total = peak + jnp.log(exp_total)
    keep = lax.broadcasted_iota(jnp.int32, (1, LANES), 1) < length_ref[0]
    logprob_ref[...] = jnp.where(keep, picked - log_total, 0.0)
    entropy_ref[...] = jnp.where(keep, log_total - exp_spread / exp_total, 0.0)


def merge(lengths, lines):
    vmem = pl.BlockSpec(memory_space=pltpu.VMEM)
    shape = jax.ShapeDtypeStruct((1, LANES), jnp.float32)
    return pl.pallas_call(
        merge_kernel,
        out_shape=(shape, shape),
        in_specs=[pl.BlockSpec(memory_space=pltpu.SMEM), vmem],
        out_specs=(vmem, vmem),
        name="merge",
    )(lengths, lines)


def places():
    z, x, core = lax.axis_index("z"), lax.axis_index("x"), lax.axis_index("core")
    near = jnp.array([0, -1, 1, -2], jnp.int32)
    far = jnp.array([2, -3, 3, -4], jnp.int32)

    def line(dz, dx, zoff):
        first = (((z + dz) % 8) * 4 + (x + near) % 4) * 2
        second = (((z + zoff) % 8) * 4 + (x + dx) % 4) * 2 + 1
        return jnp.where(core == 0, first, second)

    return jnp.concatenate(
        [
            line(0, 0, near),
            line(-1, -1, near), line(1, 1, near),
            line(-2, -1, far), line(2, 1, far),
            line(-3, -2, near), line(3, 2, far),
            line(-4, 0, far),
        ]
    ).astype(jnp.int32)


def local(hidden, gain, head_weight, token_ids, lengths, owner_device):
    core = lax.axis_index("core")
    first_core = core == 0
    cols = head_weight.shape[1]
    other_weight = lax.ppermute(head_weight, "core", [(0, 1), (1, 0)])
    chip = (lax.axis_index("z") * 4 + lax.axis_index("x")) * 2
    base = lambda c: ((chip + c) * 4 + lax.axis_index("tp")) * cols
    bases = jnp.stack([base(core), base(1 - core)]).astype(jnp.int32)

    gathered = lax.all_gather(hidden, "tp", axis=1, tiled=True)
    values = gathered.astype(jnp.float32)
    mean_square = jnp.mean(values * values, axis=-1, keepdims=True)
    normed = (values * lax.rsqrt(mean_square + 1e-05) * gain).astype(jnp.bfloat16)
    ids = token_ids[:, None]
    lane = lax.broadcasted_iota(jnp.int32, (ids.shape[0], LANES), 1)
    digits = jnp.where(lane == 0, ids >> 12, jnp.where(lane == 1, (ids >> 6) & 63, jnp.where(lane == 2, ids & 63, 0)))
    own = jnp.concatenate([normed, digits.astype(jnp.bfloat16)], axis=1)

    f1, b1 = send(own, "x", "z", 1), send(own, "x", "z", -1)
    f2, b2 = send(f1, "x", "z", 1), send(b1, None, "z", -1)
    near = jnp.concatenate([own, f1, b1, f2], axis=0)
    f3, b3 = send(f2, None, "z", 1), send(b2, None, "z", -1)
    f4 = send(f3, None, "z", 1)
    far = jnp.concatenate([b2, f3, b3, f4], axis=0)

    f_1, b_1 = send(near, "z", "x", 1), send(near, "z", "x", -1)
    f_2 = send(jnp.where(first_core, f_1, far), "z", "x", 1)
    b_2 = send(jnp.where(first_core, b_1, far), "z", "x", -1)
    f_3 = send(jnp.where(first_core, f_2, f_1), "z", "x", 1)
    b_3 = send(b_2, "z", "x", -1)
    f_4, b_4 = send(f_3[:64], "z", None, 1), send(b_3[64:], "z", None, -1)
    last = jnp.where(first_core, jnp.concatenate([f_4, b_4], axis=0), far)

    both = (head_weight, other_weight)
    lines = [
        score([near], *both, bases),
        score([f_1, b_1], *both, bases),
        score([f_2, b_2], *both, bases),
        score([f_3, b_3], *both, bases),
        score([last], *both, bases),
    ]
    dealt = deal_lines(places(), owner_device, lines, SIZES["tp"])
    met = lax.all_to_all(dealt, ALL, 0, 0, tiled=True)
    logprob, entropy = merge(lengths, met)
    slots = hidden.shape[0]
    return logprob[0, :slots], entropy[0, :slots]


def solution(mesh):
    split = Mesh(mesh.devices.reshape(8, 4, 2, 4), ALL)
    req = ("z", "x", "core")
    placed = (P(req, "tp"), P(), P(None, ALL), P(req), P(req), P())
    return jax.shard_map(local, mesh=split, in_specs=placed, out_specs=(P(req), P(req)), check_vma=False)
```

```python
import functools

import jax
import jax.numpy as jnp
from jax import lax
from jax.experimental import pallas as pl
from jax.experimental.pallas import tpu as pltpu
from jax.sharding import Mesh
from jax.sharding import PartitionSpec as P


ALL = ("zh", "zl", "x", "core", "tp")
REQ = ("zh", "zl", "x", "core")
SPLIT = (2, 4, 4, 2, 4)
LANES = 128


def pairs(step, swap):
    out = []
    for z in range(8):
        for x in range(4):
            for core in range(2):
                along_z = (core == 0) != swap
                nz = (z + step) % 8 if along_z else z
                nx = x if along_z else (x + step) % 4
                out.append(((z * 4 + x) * 2 + core, (nz * 4 + nx) * 2 + core))
    return out


def send(value, step, swap):
    return lax.ppermute(value, REQ, pairs(step, swap))


def norm_kernel(eps, blocks_ref, gain_ref, out_ref):
    halves, quarters = 2, blocks_ref.shape[0] // 2
    rows, width = blocks_ref.shape[1], gain_ref.shape[1] // quarters
    for h in range(halves):
        at = slice(h * rows, (h + 1) * rows)
        square = jnp.zeros((rows, 1), jnp.float32)
        for q in range(quarters):
            values = blocks_ref[h * quarters + q, :, :width].astype(jnp.float32)
            square += jnp.sum(values * values, axis=1, keepdims=True)
        scale = lax.rsqrt(square / (width * quarters) + eps)
        for q in range(quarters):
            values = blocks_ref[h * quarters + q, :, :width].astype(jnp.float32)
            columns = slice(q * width, (q + 1) * width)
            out_ref[at, columns] = (values * scale * gain_ref[:, columns]).astype(jnp.bfloat16)
        out_ref[at, quarters * width :] = blocks_ref[h * quarters, :, width:]


def norm(blocks, gain):
    vmem = pl.BlockSpec(memory_space=pltpu.VMEM)
    return pl.pallas_call(
        functools.partial(norm_kernel, 1e-05),
        out_shape=jax.ShapeDtypeStruct((2 * blocks.shape[1], gain.shape[0] + LANES), jnp.bfloat16),
        in_specs=[vmem, vmem],
        out_specs=vmem,
        compiler_params=pltpu.CompilerParams(vmem_limit_bytes=8 << 20),
        name="norm",
    )(blocks, gain[None, :])


def score_kernel(n_parts, width, base_ref, *refs):
    parts, (w_own, w_other, out_ref, logits) = refs[:n_parts], refs[n_parts:]
    rows = parts[0].shape[0]
    cols = w_own.shape[1]
    tile = 256
    for half, w in enumerate((w_own, w_other)):

        def column_tile(n, carry, half=half, w=w):
            at = pl.multiple_of(n * tile, tile)
            lhs = jnp.concatenate([part[:, :width] for part in parts], axis=0)
            product = jnp.dot(lhs, w[:, pl.ds(at, tile)], preferred_element_type=jnp.float32)
            logits[:, pl.ds(pl.multiple_of(half * cols + n * tile, tile), tile)] = product
            return carry

        lax.fori_loop(0, cols // tile, column_tile, 0)

    lane = lax.broadcasted_iota(jnp.int32, (32, LANES), 1)
    slot = lax.broadcasted_iota(jnp.int32, (32, LANES), 0)
    column = lax.broadcasted_iota(jnp.int32, (32, 2 * cols), 1)
    vocab = jnp.where(column < cols, base_ref[0] + column, base_ref[1] + column - cols)
    digit = jnp.where(lane == 0, 4096.0, jnp.where(lane == 1, 64.0, jnp.where(lane == 2, 1.0, 0.0)))
    for i, part in enumerate(parts):

        def group(g, carry, i=i, part=part):
            row = pl.multiple_of(g * 32, 32)
            lg = logits[pl.ds(pl.multiple_of(i * rows + g * 32, 32), 32), :]
            code = part[pl.ds(row, 32), pl.ds(width, LANES)].astype(jnp.float32)
            ids = jnp.sum(code * digit, axis=1, keepdims=True).astype(jnp.int32)
            peak = jnp.max(lg, axis=1, keepdims=True)
            weight = jnp.exp(lg - peak)
            total = jnp.sum(weight, axis=1, keepdims=True)
            spread = jnp.sum(weight * lg, axis=1, keepdims=True)
            pick = jnp.sum(jnp.where(vocab == ids, lg, 0.0), axis=1, keepdims=True)
            stat = jnp.where(lane < 32, peak, jnp.where(lane < 64, total, jnp.where(lane < 96, spread, pick)))
            line = jnp.sum(jnp.where(lane % 32 == slot, stat, 0.0), axis=0, keepdims=True)
            out_ref[pl.ds(i * (rows // 32) + g, 1), :] = line
            return carry

        lax.fori_loop(0, rows // 32, group, 0)


def score(parts, w_own, w_other, bases):
    rows = parts[0].shape[0]
    n = len(parts)
    width = w_own.shape[0]
    cols = w_own.shape[1]
    vmem = pl.BlockSpec(memory_space=pltpu.VMEM)
    return pl.pallas_call(
        functools.partial(score_kernel, n, width),
        out_shape=jax.ShapeDtypeStruct((n * rows // 32, LANES), jnp.float32),
        in_specs=[pl.BlockSpec(memory_space=pltpu.SMEM)] + [vmem] * (n + 2),
        out_specs=vmem,
        scratch_shapes=[pltpu.VMEM((n * rows, 2 * cols), jnp.float32)],
        cost_estimate=pl.CostEstimate(
            flops=4 * n * rows * width * cols, bytes_accessed=n * rows * width * 2, transcendentals=2 * n * rows * cols
        ),
        compiler_params=pltpu.CompilerParams(vmem_limit_bytes=24 << 20),
        name="score",
    )(bases, *parts, w_own, w_other)


def table_kernel(place_ref, owner_ref, *refs):
    lines, (out_ref, table) = refs[:-2], refs[-2:]
    table[...] = jnp.zeros_like(table)
    at = 0
    for line in lines:
        for i in range(line.shape[0]):
            table[pl.ds(place_ref[at], 1), :] = line[i : i + 1, :]
            at += 1
    copies = out_ref.shape[0] // table.shape[0]

    def deal(o, carry):
        row = table[pl.ds(owner_ref[o], 1), :]
        for c in range(copies):
            out_ref[pl.ds(o * copies + c, 1), :] = row
        return carry

    lax.fori_loop(0, table.shape[0], deal, 0)


def deal_lines(place, owner, lines, copies):
    smem = pl.BlockSpec(memory_space=pltpu.SMEM)
    vmem = pl.BlockSpec(memory_space=pltpu.VMEM)
    groups = owner.shape[0]
    return pl.pallas_call(
        table_kernel,
        out_shape=jax.ShapeDtypeStruct((groups * copies, LANES), jnp.float32),
        in_specs=[smem, smem] + [vmem] * len(lines),
        out_specs=vmem,
        scratch_shapes=[pltpu.VMEM((groups, LANES), jnp.float32)],
        name="deal",
    )(place, owner, *lines)


def merge_kernel(length_ref, lines_ref, logprob_ref, entropy_ref):
    lines = lines_ref[...]
    total = pltpu.roll(lines, 96, 1)
    spread = pltpu.roll(lines, 64, 1)
    pick = pltpu.roll(lines, 32, 1)
    lane = lax.broadcasted_iota(jnp.int32, lines.shape, 1)
    live = (total > 0.0) & (lane < 32)
    peak = jnp.max(jnp.where(live, lines, -jnp.inf), axis=0, keepdims=True)
    scale = jnp.where(live, jnp.exp(lines - peak), 0.0)
    exp_total = jnp.sum(jnp.where(live, scale * total, 0.0), axis=0, keepdims=True)
    exp_spread = jnp.sum(jnp.where(live, scale * spread, 0.0), axis=0, keepdims=True)
    picked = jnp.sum(jnp.where(live, pick, 0.0), axis=0, keepdims=True)
    log_total = peak + jnp.log(exp_total)
    keep = lax.broadcasted_iota(jnp.int32, (1, LANES), 1) < length_ref[0]
    slots = logprob_ref.shape[0]
    logprob_ref[...] = jnp.where(keep, picked - log_total, 0.0)[0, :slots]
    entropy_ref[...] = jnp.where(keep, log_total - exp_spread / exp_total, 0.0)[0, :slots]


def merge(lengths, lines, slots):
    vmem = pl.BlockSpec(memory_space=pltpu.VMEM)
    shape = jax.ShapeDtypeStruct((slots,), jnp.float32)
    return pl.pallas_call(
        merge_kernel,
        out_shape=(shape, shape),
        in_specs=[pl.BlockSpec(memory_space=pltpu.SMEM), vmem],
        out_specs=(vmem, vmem),
        name="merge",
    )(lengths, lines)


def places():
    zl, x, core = lax.axis_index("zl"), lax.axis_index("x"), lax.axis_index("core")
    outer, inner = jnp.where(core == 0, zl, x), jnp.where(core == 0, x, zl)

    def line(step, offsets):
        far = (outer + step) % 4
        out = []
        for offset in offsets:
            near = (inner + offset) % 4
            z, col = jnp.where(core == 0, far, near), jnp.where(core == 0, near, far)
            out += [((half * 4 + z) * 4 + col) * 2 + core for half in range(2)]
        return out

    first, second = (0, 3), (1, 2)
    order = [(0, first), (0, second), (3, first), (1, first), (3, second), (1, second), (2, first), (2, second)]
    return jnp.stack([w for step, offsets in order for w in line(step, offsets)]).astype(jnp.int32)


def local(hidden, gain, head_weight, token_ids, lengths, owner_device):
    core = lax.axis_index("core")
    cols, slots = head_weight.shape[1], hidden.shape[0]
    other_weight = lax.ppermute(head_weight, "core", [(0, 1), (1, 0)])
    chip = ((lax.axis_index("zh") * 4 + lax.axis_index("zl")) * 4 + lax.axis_index("x")) * 2
    base = lambda c: ((chip + c) * 4 + lax.axis_index("tp")) * cols
    bases = jnp.stack([base(core), base(1 - core)]).astype(jnp.int32)

    ids = token_ids[:, None]
    lane = lax.broadcasted_iota(jnp.int32, (slots, LANES), 1)
    digits = jnp.where(lane == 0, ids >> 12, jnp.where(lane == 1, (ids >> 6) & 63, jnp.where(lane == 2, ids & 63, 0)))
    block = jnp.concatenate([hidden, digits.astype(jnp.bfloat16)], axis=1)
    blocks = lax.all_to_all(jnp.broadcast_to(block[None], (8, *block.shape)), ("zh", "tp"), 0, 0, tiled=True)
    own = norm(blocks, gain)

    f1, b1 = send(own, 1, True), send(own, -1, True)
    first = jnp.concatenate([own, f1], axis=0)
    f2, b2 = send(f1[:slots], 1, True), send(b1[slots:], -1, True)
    second = jnp.concatenate([b1, f2, b2], axis=0)
    first, other_weight = lax.optimization_barrier((first, other_weight))
    fa, ba = send(first, 1, False), send(first, -1, False)
    fb, bb = send(second, 1, False), send(second, -1, False)
    oa, ob = send(fa, 1, False), send(bb, -1, False)

    both = (head_weight, other_weight)
    lines = [score(parts, *both, bases) for parts in ([first, second], [fa, ba], [fb, bb], [oa, ob])]
    dealt = deal_lines(places(), owner_device, lines, 4)
    met = lax.all_to_all(dealt, ALL, 0, 0, tiled=True)
    return merge(lengths, met, slots)


def solution(mesh):
    split = Mesh(mesh.devices.reshape(SPLIT), ALL)
    placed = (P(REQ, "tp"), P(), P(None, ALL), P(REQ), P(REQ), P())
    return jax.shard_map(local, mesh=split, in_specs=placed, out_specs=(P(REQ), P(REQ)), check_vma=False)
```

```python
import functools

import jax
import jax.numpy as jnp
from jax import lax
from jax.experimental import pallas as pl
from jax.experimental.pallas import tpu as pltpu
from jax.sharding import Mesh
from jax.sharding import PartitionSpec as P


ALL = ("zh", "zl", "x", "core", "tp")
REQ = ("zh", "zl", "x", "core")
SPLIT = (2, 4, 4, 2, 4)
LANES = 128


def pairs(step, swap):
    out = []
    for z in range(8):
        for x in range(4):
            for core in range(2):
                along_z = (core == 0) != swap
                nz = (z + step) % 8 if along_z else z
                nx = x if along_z else (x + step) % 4
                out.append(((z * 4 + x) * 2 + core, (nz * 4 + nx) * 2 + core))
    return out


def send(value, step, swap):
    return lax.ppermute(value, REQ, pairs(step, swap))


def norm_kernel(eps, spot_ref, *refs):
    pieces, (gain_ref, out_ref) = refs[:-2], refs[-2:]
    width, quarters = gain_ref.shape[1] // 4, 4
    rows = pieces[0].shape[0]
    for h in range(2):
        mine = pieces[h * quarters : (h + 1) * quarters]
        at = pl.ds(pl.multiple_of(spot_ref[h] * rows, rows), rows)
        square = jnp.zeros((rows, 1), jnp.float32)
        for piece in mine:
            values = piece[:, :width].astype(jnp.float32)
            square += jnp.sum(values * values, axis=1, keepdims=True)
        scale = lax.rsqrt(square / (width * quarters) + eps)
        for q, piece in enumerate(mine):
            columns = pl.ds(pl.multiple_of(spot_ref[2 + q] * width, LANES), width)
            values = piece[:, :width].astype(jnp.float32)
            out_ref[at, columns] = (values * scale * gain_ref[:, columns]).astype(jnp.bfloat16)
        out_ref[at, quarters * width :] = mine[0][:, width:]


def norm(spots, pieces, gain):
    vmem = pl.BlockSpec(memory_space=pltpu.VMEM)
    return pl.pallas_call(
        functools.partial(norm_kernel, 1e-05),
        out_shape=jax.ShapeDtypeStruct((2 * pieces[0].shape[0], gain.shape[0] + LANES), jnp.bfloat16),
        in_specs=[pl.BlockSpec(memory_space=pltpu.SMEM)] + [vmem] * (len(pieces) + 1),
        out_specs=vmem,
        compiler_params=pltpu.CompilerParams(vmem_limit_bytes=4 << 20),
        name="norm",
    )(spots, *pieces, gain[None, :])


def score_kernel(n_parts, width, base_ref, *refs):
    parts, (w_own, w_other, out_ref, logits) = refs[:n_parts], refs[n_parts:]
    rows = parts[0].shape[0]
    cols = w_own.shape[1]
    tile = 256
    for half, w in enumerate((w_own, w_other)):

        def column_tile(n, carry, half=half, w=w):
            at = pl.multiple_of(n * tile, tile)
            lhs = jnp.concatenate([part[:, :width] for part in parts], axis=0)
            product = jnp.dot(lhs, w[:, pl.ds(at, tile)], preferred_element_type=jnp.float32)
            logits[:, pl.ds(pl.multiple_of(half * cols + n * tile, tile), tile)] = product
            return carry

        lax.fori_loop(0, cols // tile, column_tile, 0)

    lane = lax.broadcasted_iota(jnp.int32, (32, LANES), 1)
    slot = lax.broadcasted_iota(jnp.int32, (32, LANES), 0)
    column = lax.broadcasted_iota(jnp.int32, (32, 2 * cols), 1)
    vocab = jnp.where(column < cols, base_ref[0] + column, base_ref[1] + column - cols)
    digit = jnp.where(lane == 0, 4096.0, jnp.where(lane == 1, 64.0, jnp.where(lane == 2, 1.0, 0.0)))
    for i, part in enumerate(parts):

        def group(g, carry, i=i, part=part):
            row = pl.multiple_of(g * 32, 32)
            lg = logits[pl.ds(pl.multiple_of(i * rows + g * 32, 32), 32), :]
            code = part[pl.ds(row, 32), pl.ds(width, LANES)].astype(jnp.float32)
            ids = jnp.sum(code * digit, axis=1, keepdims=True).astype(jnp.int32)
            peak = jnp.max(lg, axis=1, keepdims=True)
            weight = jnp.exp(lg - peak)
            total = jnp.sum(weight, axis=1, keepdims=True)
            spread = jnp.sum(weight * lg, axis=1, keepdims=True)
            pick = jnp.sum(jnp.where(vocab == ids, lg, 0.0), axis=1, keepdims=True)
            stat = jnp.where(lane < 32, peak, jnp.where(lane < 64, total, jnp.where(lane < 96, spread, pick)))
            line = jnp.sum(jnp.where(lane % 32 == slot, stat, 0.0), axis=0, keepdims=True)
            out_ref[pl.ds(i * (rows // 32) + g, 1), :] = line
            return carry

        lax.fori_loop(0, rows // 32, group, 0)


def score(parts, w_own, w_other, bases):
    rows = parts[0].shape[0]
    n = len(parts)
    width = w_own.shape[0]
    cols = w_own.shape[1]
    vmem = pl.BlockSpec(memory_space=pltpu.VMEM)
    return pl.pallas_call(
        functools.partial(score_kernel, n, width),
        out_shape=jax.ShapeDtypeStruct((n * rows // 32, LANES), jnp.float32),
        in_specs=[pl.BlockSpec(memory_space=pltpu.SMEM)] + [vmem] * (n + 2),
        out_specs=vmem,
        scratch_shapes=[pltpu.VMEM((n * rows, 2 * cols), jnp.float32)],
        cost_estimate=pl.CostEstimate(
            flops=4 * n * rows * width * cols, bytes_accessed=n * rows * width * 2, transcendentals=2 * n * rows * cols
        ),
        compiler_params=pltpu.CompilerParams(vmem_limit_bytes=16 << 20),
        name="score",
    )(bases, *parts, w_own, w_other)


def table_kernel(place_ref, owner_ref, *refs):
    lines, (out_ref, table) = refs[:-2], refs[-2:]
    table[...] = jnp.zeros_like(table)
    at = 0
    for line in lines:
        for i in range(line.shape[0]):
            table[pl.ds(place_ref[at], 1), :] = line[i : i + 1, :]
            at += 1
    copies = out_ref.shape[0] // table.shape[0]

    def deal(o, carry):
        row = table[pl.ds(owner_ref[o], 1), :]
        for c in range(copies):
            out_ref[pl.ds(o * copies + c, 1), :] = row
        return carry

    lax.fori_loop(0, table.shape[0], deal, 0)


def deal_lines(place, owner, lines, copies):
    smem = pl.BlockSpec(memory_space=pltpu.SMEM)
    vmem = pl.BlockSpec(memory_space=pltpu.VMEM)
    groups = owner.shape[0]
    return pl.pallas_call(
        table_kernel,
        out_shape=jax.ShapeDtypeStruct((groups * copies, LANES), jnp.float32),
        in_specs=[smem, smem] + [vmem] * len(lines),
        out_specs=vmem,
        scratch_shapes=[pltpu.VMEM((groups, LANES), jnp.float32)],
        compiler_params=pltpu.CompilerParams(vmem_limit_bytes=2 << 20),
        name="deal",
    )(place, owner, *lines)


def merge_kernel(length_ref, lines_ref, logprob_ref, entropy_ref):
    lines = lines_ref[...]
    total = pltpu.roll(lines, 96, 1)
    spread = pltpu.roll(lines, 64, 1)
    pick = pltpu.roll(lines, 32, 1)
    lane = lax.broadcasted_iota(jnp.int32, lines.shape, 1)
    live = (total > 0.0) & (lane < 32)
    peak = jnp.max(jnp.where(live, lines, -jnp.inf), axis=0, keepdims=True)
    scale = jnp.where(live, jnp.exp(lines - peak), 0.0)
    exp_total = jnp.sum(jnp.where(live, scale * total, 0.0), axis=0, keepdims=True)
    exp_spread = jnp.sum(jnp.where(live, scale * spread, 0.0), axis=0, keepdims=True)
    picked = jnp.sum(jnp.where(live, pick, 0.0), axis=0, keepdims=True)
    log_total = peak + jnp.log(exp_total)
    keep = lax.broadcasted_iota(jnp.int32, (1, LANES), 1) < length_ref[0]
    slots = logprob_ref.shape[0]
    logprob_ref[...] = jnp.where(keep, picked - log_total, 0.0)[0, :slots]
    entropy_ref[...] = jnp.where(keep, log_total - exp_spread / exp_total, 0.0)[0, :slots]


def merge(lengths, lines, slots):
    vmem = pl.BlockSpec(memory_space=pltpu.VMEM)
    shape = jax.ShapeDtypeStruct((slots,), jnp.float32)
    return pl.pallas_call(
        merge_kernel,
        out_shape=(shape, shape),
        in_specs=[pl.BlockSpec(memory_space=pltpu.SMEM), vmem],
        out_specs=(vmem, vmem),
        compiler_params=pltpu.CompilerParams(vmem_limit_bytes=4 << 20),
        name="merge",
    )(lengths, lines)


def places():
    zl, x, core = lax.axis_index("zl"), lax.axis_index("x"), lax.axis_index("core")
    outer, inner = jnp.where(core == 0, zl, x), jnp.where(core == 0, x, zl)

    def line(step, offset, halves):
        far, near = (outer + step) % 4, (inner + offset) % 4
        z, col = jnp.where(core == 0, far, near), jnp.where(core == 0, near, far)
        return [((half * 4 + z) * 4 + col) * 2 + core for half in halves]

    both = (0, 1)
    order = [(0, o) for o in (0, 3, 1, 2)] + [(3, 0), (3, 3), (1, 0), (1, 3)]
    order += [(3, 1), (3, 2), (1, 1), (1, 2), (2, 0), (2, 3), (2, 1), (2, 2)]
    return jnp.stack([w for step, offset in order for w in line(step, offset, both)]).astype(jnp.int32)


def local(hidden, gain, head_weight, token_ids, lengths, owner_device):
    core = lax.axis_index("core")
    cols, slots = head_weight.shape[1], hidden.shape[0]
    other_weight = lax.ppermute(head_weight, "core", [(0, 1), (1, 0)])
    chip = ((lax.axis_index("zh") * 4 + lax.axis_index("zl")) * 4 + lax.axis_index("x")) * 2
    base = lambda c: ((chip + c) * 4 + lax.axis_index("tp")) * cols
    bases = jnp.stack([base(core), base(1 - core)]).astype(jnp.int32)

    ids = token_ids[:, None]
    lane = lax.broadcasted_iota(jnp.int32, (slots, LANES), 1)
    digits = jnp.where(lane == 0, ids >> 12, jnp.where(lane == 1, (ids >> 6) & 63, jnp.where(lane == 2, ids & 63, 0)))
    block = jnp.concatenate([hidden, digits.astype(jnp.bfloat16)], axis=1)
    partner = lax.ppermute(block, "zh", [(0, 1), (1, 0)])
    around = lambda value: [value] + [lax.ppermute(value, "tp", [(i, (i - k) % 4) for i in range(4)]) for k in (1, 3, 2)]
    half, quarter = lax.axis_index("zh"), lax.axis_index("tp")
    spots = jnp.stack([half, 1 - half] + [(quarter + k) % 4 for k in (0, 1, 3, 2)]).astype(jnp.int32)
    own = norm(spots, around(block) + around(partner), gain)
    own, other_weight = lax.optimization_barrier((own, other_weight))

    both = (head_weight, other_weight)
    lines = ring(own, both, bases, slots)
    dealt = deal_lines(places(), owner_device, lines, 4)
    met = lax.all_to_all(dealt, ALL, 0, 0, tiled=True)
    return merge(lengths, met, slots)


def ring(own, both, bases, slots):
    def move(value, step, swap=False):
        return send(value, step, swap)

    def scored(parts):
        return score(parts, *both, bases)

    f1, b1 = move(own, 1, True), move(own, -1, True)
    first = jnp.concatenate([own, f1], axis=0)
    fa, ba = move(first, 1), move(first, -1)
    f2, b2 = move(f1[:slots], 1, True), move(b1[slots:], -1, True)
    second = jnp.concatenate([b1, f2, b2], axis=0)
    fb, bb = move(second, 1), move(second, -1)
    rows = slots * 2
    fc, bc = move(fa[:rows], 1), move(ba[rows:], -1)
    fd, bd = move(fb[:rows], 1), move(bb[rows:], -1)
    return [scored([first, second]), scored([fa, ba]), scored([fb, bb]), scored([fc, bc]), scored([fd, bd])]


def solution(mesh):
    split = Mesh(mesh.devices.reshape(SPLIT), ALL)
    placed = (P(REQ, "tp"), P(), P(None, ALL), P(REQ), P(REQ), P())
    return jax.shard_map(local, mesh=split, in_specs=placed, out_specs=(P(REQ), P(REQ)), check_vma=False)
```

```python
import functools

import jax
import jax.numpy as jnp
import numpy as np
from jax import lax
from jax.experimental import pallas as pl
from jax.experimental.pallas import tpu as pltpu
from jax.sharding import Mesh
from jax.sharding import PartitionSpec as P


ALL = ("zh", "zl", "x", "core", "tp")
REQ = ("zh", "zl", "x", "core")
SPLIT = (2, 4, 4, 2, 4)
LANES = 128


def pairs(step, swap):
    out = []
    for z in range(8):
        for x in range(4):
            for core in range(2):
                along_z = (core == 0) != swap
                nz = (z + step) % 8 if along_z else z
                nx = x if along_z else (x + step) % 4
                out.append(((z * 4 + x) * 2 + core, (nz * 4 + nx) * 2 + core))
    return out


def send(value, step, swap):
    return lax.ppermute(value, REQ, pairs(step, swap))


def norm_kernel(eps, spot_ref, *refs):
    pieces, (gain_ref, out_ref) = refs[:-2], refs[-2:]
    width, quarters = gain_ref.shape[1] // 4, 4
    rows = pieces[0].shape[0]
    for h in range(2):
        mine = pieces[h * quarters : (h + 1) * quarters]
        at = pl.ds(pl.multiple_of(spot_ref[PLACES + h] * rows, rows), rows)
        square = jnp.zeros((rows, 1), jnp.float32)
        for piece in mine:
            values = piece[:, :width].astype(jnp.float32)
            square += jnp.sum(values * values, axis=1, keepdims=True)
        scale = lax.rsqrt(square / (width * quarters) + eps)
        for q, piece in enumerate(mine):
            columns = pl.ds(pl.multiple_of(spot_ref[PLACES + 2 + q] * width, LANES), width)
            values = piece[:, :width].astype(jnp.float32)
            out_ref[at, columns] = (values * scale * gain_ref[:, columns]).astype(jnp.bfloat16)
        out_ref[at, quarters * width :] = mine[0][:, width:]


def norm(spots, pieces, gain):
    vmem = pl.BlockSpec(memory_space=pltpu.VMEM)
    return pl.pallas_call(
        functools.partial(norm_kernel, 1e-05),
        out_shape=jax.ShapeDtypeStruct((2 * pieces[0].shape[0], gain.shape[0] + LANES), jnp.bfloat16),
        in_specs=[pl.BlockSpec(memory_space=pltpu.SMEM)] + [vmem] * (len(pieces) + 1),
        out_specs=vmem,
        compiler_params=pltpu.CompilerParams(vmem_limit_bytes=4 << 20),
        name="norm",
    )(spots, *pieces, gain[None, :])


TILE = 256


def score_kernel(sizes, width, base_ref, *refs):
    n = len(sizes)
    parts, (w_own, w_other, out_ref, logits, weights, sems) = refs[:n], refs[n:]
    cols = w_own.shape[1]
    per_half = cols // TILE

    def fetch(half, n):
        source = (w_own, w_other)[half].at[:, pl.ds(n * TILE, TILE)]
        slot = half * per_half + n
        return pltpu.make_async_copy(source, weights.at[slot], sems.at[slot])

    for half in range(2):
        for i in range(per_half):
            fetch(half, i).start()

    def column_tile(slot, carry):
        pltpu.make_async_copy(w_own.at[:, pl.ds(0, TILE)], weights.at[slot], sems.at[slot]).wait()
        lhs = jnp.concatenate([part[:, :width] for part in parts], axis=0)
        product = jnp.dot(lhs, weights[slot], preferred_element_type=jnp.float32)
        logits[:, pl.ds(pl.multiple_of(slot * TILE, TILE), TILE)] = product
        return carry

    lax.fori_loop(0, 2 * per_half, column_tile, 0)

    lane = lax.broadcasted_iota(jnp.int32, (32, LANES), 1)
    slot = lax.broadcasted_iota(jnp.int32, (32, LANES), 0)
    column = lax.broadcasted_iota(jnp.int32, (32, 2 * cols), 1)
    first_base, second_base = (base_ref[PLACES + SPOTS + i] * cols for i in range(2))
    vocab = jnp.where(column < cols, first_base + column, second_base + column - cols)
    digit = jnp.where(lane == 0, 4096.0, jnp.where(lane == 1, 64.0, jnp.where(lane == 2, 1.0, 0.0)))
    before = 0
    for part, rows in zip(parts, sizes):

        def group(g, carry, part=part, before=before):
            row = pl.multiple_of(g * 32, 32)
            lg = logits[pl.ds(pl.multiple_of(before + g * 32, 32), 32), :]
            code = part[pl.ds(row, 32), pl.ds(width, LANES)].astype(jnp.float32)
            ids = jnp.sum(code * digit, axis=1, keepdims=True).astype(jnp.int32)
            peak = jnp.max(lg, axis=1, keepdims=True)
            weight = jnp.exp(lg - peak)
            total = jnp.sum(weight, axis=1, keepdims=True)
            spread = jnp.sum(weight * lg, axis=1, keepdims=True)
            pick = jnp.sum(jnp.where(vocab == ids, lg, 0.0), axis=1, keepdims=True)
            stat = jnp.where(lane < 32, peak, jnp.where(lane < 64, total, jnp.where(lane < 96, spread, pick)))
            line = jnp.sum(jnp.where(lane % 32 == slot, stat, 0.0), axis=0, keepdims=True)
            out_ref[pl.ds(before // 32 + g, 1), :] = line
            return carry

        lax.fori_loop(0, rows // 32, group, 0)
        before += rows


def score(parts, w_own, w_other, bases):
    sizes = tuple(part.shape[0] for part in parts)
    rows = sum(sizes)
    width, cols = w_own.shape
    vmem = pl.BlockSpec(memory_space=pltpu.VMEM)
    hbm = pl.BlockSpec(memory_space=pltpu.HBM)
    return pl.pallas_call(
        functools.partial(score_kernel, sizes, width),
        out_shape=jax.ShapeDtypeStruct((rows // 32, LANES), jnp.float32),
        in_specs=[pl.BlockSpec(memory_space=pltpu.SMEM)] + [vmem] * len(parts) + [hbm, hbm],
        out_specs=vmem,
        scratch_shapes=[
            pltpu.VMEM((rows, 2 * cols), jnp.float32),
            pltpu.VMEM((2 * cols // TILE, width, TILE), jnp.bfloat16),
            pltpu.SemaphoreType.DMA((2 * cols // TILE,)),
        ],
        cost_estimate=pl.CostEstimate(
            flops=4 * rows * width * cols, bytes_accessed=4 * width * cols, transcendentals=2 * rows * cols
        ),
        compiler_params=pltpu.CompilerParams(vmem_limit_bytes=22 << 20),
        name="score",
    )(bases, *parts, w_own, w_other)


def table_kernel(place_ref, owner_ref, *refs):
    lines, (out_ref, table) = refs[:-2], refs[-2:]
    table[...] = jnp.zeros_like(table)
    at = 0
    for line in lines:
        for i in range(line.shape[0]):
            table[pl.ds(place_ref[at], 1), :] = line[i : i + 1, :]
            at += 1
    copies = out_ref.shape[0] // table.shape[0]

    def deal(o, carry):
        row = table[pl.ds(owner_ref[o], 1), :]
        for c in range(copies):
            out_ref[pl.ds(o * copies + c, 1), :] = row
        return carry

    lax.fori_loop(0, table.shape[0], deal, 0, unroll=8)


def deal_lines(place, owner, lines, copies):
    smem = pl.BlockSpec(memory_space=pltpu.SMEM)
    vmem = pl.BlockSpec(memory_space=pltpu.VMEM)
    groups = owner.shape[0]
    return pl.pallas_call(
        table_kernel,
        out_shape=jax.ShapeDtypeStruct((groups * copies, LANES), jnp.float32),
        in_specs=[smem, smem] + [vmem] * len(lines),
        out_specs=vmem,
        scratch_shapes=[pltpu.VMEM((groups, LANES), jnp.float32)],
        compiler_params=pltpu.CompilerParams(vmem_limit_bytes=2 << 20),
        name="deal",
    )(place, owner, *lines)


def merge_kernel(length_ref, lines_ref, logprob_ref, entropy_ref):
    lines = lines_ref[...]
    total = pltpu.roll(lines, 96, 1)
    spread = pltpu.roll(lines, 64, 1)
    pick = pltpu.roll(lines, 32, 1)
    lane = lax.broadcasted_iota(jnp.int32, lines.shape, 1)
    live = (total > 0.0) & (lane < 32)
    peak = jnp.max(jnp.where(live, lines, -jnp.inf), axis=0, keepdims=True)
    scale = jnp.where(live, jnp.exp(lines - peak), 0.0)
    exp_total = jnp.sum(jnp.where(live, scale * total, 0.0), axis=0, keepdims=True)
    exp_spread = jnp.sum(jnp.where(live, scale * spread, 0.0), axis=0, keepdims=True)
    picked = jnp.sum(jnp.where(live, pick, 0.0), axis=0, keepdims=True)
    log_total = peak + jnp.log(exp_total)
    keep = lax.broadcasted_iota(jnp.int32, (1, LANES), 1) < length_ref[0]
    slots = logprob_ref.shape[0]
    logprob_ref[...] = jnp.where(keep, picked - log_total, 0.0)[0, :slots]
    entropy_ref[...] = jnp.where(keep, log_total - exp_spread / exp_total, 0.0)[0, :slots]


def merge(lengths, lines, slots):
    vmem = pl.BlockSpec(memory_space=pltpu.VMEM)
    shape = jax.ShapeDtypeStruct((slots,), jnp.float32)
    return pl.pallas_call(
        merge_kernel,
        out_shape=(shape, shape),
        in_specs=[pl.BlockSpec(memory_space=pltpu.SMEM), vmem],
        out_specs=(vmem, vmem),
        compiler_params=pltpu.CompilerParams(vmem_limit_bytes=4 << 20),
        name="merge",
    )(lengths, lines)


PLACES, SPOTS = 32, 6


def guide():
    table = np.zeros((8, 4, 2, 4, PLACES + SPOTS + 2), np.int32)
    order = [(0, o) for o in (0, 3, 1, 2)] + [(3, 0), (3, 3), (1, 0), (1, 3)]
    order += [(3, 1), (3, 2), (1, 1), (1, 2), (2, 0), (2, 3), (2, 1), (2, 2)]
    for z, x, core, tp in np.ndindex(8, 4, 2, 4):
        outer, inner = (z % 4, x) if core == 0 else (x, z % 4)
        row = []
        for step, offset in order:
            far, near = (outer + step) % 4, (inner + offset) % 4
            at_z, at_x = (far, near) if core == 0 else (near, far)
            row += [((half * 4 + at_z) * 4 + at_x) * 2 + core for half in range(2)]
        row += [z // 4, 1 - z // 4] + [(tp + k) % 4 for k in (0, 1, 3, 2)]
        row += [((z * 4 + x) * 2 + c) * 4 + tp for c in (core, 1 - core)]
        table[z, x, core, tp] = row
    return jnp.asarray(table.reshape(256, -1))


def local(hidden, gain, head_weight, token_ids, lengths, owner_device):
    slots = hidden.shape[0]
    device = lax.axis_index(ALL)
    index = lax.dynamic_index_in_dim(guide(), device, 0, keepdims=False)
    other_weight = lax.ppermute(head_weight, "core", [(0, 1), (1, 0)])

    ids = token_ids[:, None]
    lane = lax.broadcasted_iota(jnp.int32, (slots, LANES), 1)
    digits = jnp.where(lane == 0, ids >> 12, jnp.where(lane == 1, (ids >> 6) & 63, jnp.where(lane == 2, ids & 63, 0)))
    block = jnp.concatenate([hidden, digits.astype(jnp.bfloat16)], axis=1)
    block, index = lax.optimization_barrier((block, index))
    partner = lax.ppermute(block, "zh", [(0, 1), (1, 0)])
    around = lambda value: [value] + [lax.ppermute(value, "tp", [(i, (i - k) % 4) for i in range(4)]) for k in (1, 3, 2)]
    own = norm(index, around(block) + around(partner), gain)
    own, other_weight = lax.optimization_barrier((own, other_weight))

    both = (head_weight, other_weight)
    lines = ring(own, both, index, slots)
    dealt = deal_lines(index, owner_device, lines, 4)
    met = lax.all_to_all(dealt, ALL, 0, 0, tiled=True)
    return merge(lengths, met, slots)


def ring(own, both, index, slots):
    def move(value, step, swap=False):
        return send(value, step, swap)

    def scored(parts):
        return score(parts, *both, index)

    f1, b1 = move(own, 1, True), move(own, -1, True)
    first = jnp.concatenate([own, f1], axis=0)
    fa, ba = move(first, 1), move(first, -1)
    f2, b2 = move(f1[:slots], 1, True), move(b1[slots:], -1, True)
    second = jnp.concatenate([b1, f2, b2], axis=0)
    fb, bb = move(second, 1), move(second, -1)
    rows = slots * 2
    fc, bc = move(fa[:rows], 1), move(ba[rows:], -1)
    fd, bd = move(fb[:rows], 1), move(bb[rows:], -1)
    return [scored([first, second, fa, ba]), scored([fb, bb, fc, bc]), scored([fd, bd])]


def solution(mesh):
    split = Mesh(mesh.devices.reshape(SPLIT), ALL)
    placed = (P(REQ, "tp"), P(), P(None, ALL), P(REQ), P(REQ), P())
    return jax.shard_map(local, mesh=split, in_specs=placed, out_specs=(P(REQ), P(REQ)), check_vma=False)
```

```python
import functools

import jax
import jax.numpy as jnp
import numpy as np
from jax import lax
from jax.experimental import pallas as pl
from jax.experimental.pallas import tpu as pltpu
from jax.sharding import Mesh
from jax.sharding import PartitionSpec as P


ALL = ("zh", "zl", "x", "core", "tp")
REQ = ("zh", "zl", "x", "core")
SPLIT = (2, 4, 4, 2, 4)
LANES = 128


def pairs(step, swap):
    out = []
    for z in range(8):
        for x in range(4):
            for core in range(2):
                along_z = (core == 0) != swap
                nz = (z + step) % 8 if along_z else z
                nx = x if along_z else (x + step) % 4
                out.append(((z * 4 + x) * 2 + core, (nz * 4 + nx) * 2 + core))
    return out


def send(value, step, swap):
    return lax.ppermute(value, REQ, pairs(step, swap))


def norm_kernel(eps, spot_ref, *refs):
    pieces, (gain_ref, out_ref) = refs[:-2], refs[-2:]
    quarters = len(pieces)
    width = gain_ref.shape[1] // quarters
    square = jnp.zeros((pieces[0].shape[0], 1), jnp.float32)
    for piece in pieces:
        values = piece[:, :width].astype(jnp.float32)
        square += jnp.sum(values * values, axis=1, keepdims=True)
    scale = lax.rsqrt(square / (width * quarters) + eps)
    for q, piece in enumerate(pieces):
        columns = pl.ds(pl.multiple_of(spot_ref[PLACES + q] * width, LANES), width)
        values = piece[:, :width].astype(jnp.float32)
        out_ref[:, columns] = (values * scale * gain_ref[:, columns]).astype(jnp.bfloat16)
    out_ref[:, quarters * width :] = pieces[0][:, width:]


def norm(spots, pieces, gain):
    vmem = pl.BlockSpec(memory_space=pltpu.VMEM)
    return pl.pallas_call(
        functools.partial(norm_kernel, 1e-05),
        out_shape=jax.ShapeDtypeStruct((pieces[0].shape[0], gain.shape[0] + LANES), jnp.bfloat16),
        in_specs=[pl.BlockSpec(memory_space=pltpu.SMEM)] + [vmem] * (len(pieces) + 1),
        out_specs=vmem,
        compiler_params=pltpu.CompilerParams(vmem_limit_bytes=4 << 20),
        name="norm",
    )(spots, *pieces, gain[None, :])


TILE = 256


def score_kernel(sizes, width, base_ref, *refs):
    n = len(sizes)
    parts, (w_own, w_other, out_ref, logits, weights, sems) = refs[:n], refs[n:]
    cols = w_own.shape[1]
    per_half = cols // TILE

    def fetch(half, n):
        source = (w_own, w_other)[half].at[:, pl.ds(n * TILE, TILE)]
        slot = half * per_half + n
        return pltpu.make_async_copy(source, weights.at[slot], sems.at[slot])

    for half in range(2):
        for i in range(per_half):
            fetch(half, i).start()

    def column_tile(slot, carry):
        pltpu.make_async_copy(w_own.at[:, pl.ds(0, TILE)], weights.at[slot], sems.at[slot]).wait()
        lhs = jnp.concatenate([part[:, :width] for part in parts], axis=0)
        product = jnp.dot(lhs, weights[slot], preferred_element_type=jnp.float32)
        logits[:, pl.ds(pl.multiple_of(slot * TILE, TILE), TILE)] = product
        return carry

    lax.fori_loop(0, 2 * per_half, column_tile, 0)

    lane = lax.broadcasted_iota(jnp.int32, (32, LANES), 1)
    slot = lax.broadcasted_iota(jnp.int32, (32, LANES), 0)
    column = lax.broadcasted_iota(jnp.int32, (32, 2 * cols), 1)
    first_base, second_base = (base_ref[PLACES + SPOTS + i] * cols for i in range(2))
    vocab = jnp.where(column < cols, first_base + column, second_base + column - cols)
    digit = jnp.where(lane == 0, 4096.0, jnp.where(lane == 1, 64.0, jnp.where(lane == 2, 1.0, 0.0)))
    before = 0
    for part, rows in zip(parts, sizes):

        def group(g, carry, part=part, before=before):
            row = pl.multiple_of(g * 32, 32)
            lg = logits[pl.ds(pl.multiple_of(before + g * 32, 32), 32), :]
            code = part[pl.ds(row, 32), pl.ds(width, LANES)].astype(jnp.float32)
            ids = jnp.sum(code * digit, axis=1, keepdims=True).astype(jnp.int32)
            peak = jnp.max(lg, axis=1, keepdims=True)
            weight = jnp.exp(lg - peak)
            total = jnp.sum(weight, axis=1, keepdims=True)
            spread = jnp.sum(weight * lg, axis=1, keepdims=True)
            pick = jnp.sum(jnp.where(vocab == ids, lg, 0.0), axis=1, keepdims=True)
            stat = jnp.where(lane < 32, peak, jnp.where(lane < 64, total, jnp.where(lane < 96, spread, pick)))
            line = jnp.sum(jnp.where(lane % 32 == slot, stat, 0.0), axis=0, keepdims=True)
            out_ref[pl.ds(before // 32 + g, 1), :] = line
            return carry

        lax.fori_loop(0, rows // 32, group, 0)
        before += rows


def score(parts, w_own, w_other, bases):
    sizes = tuple(part.shape[0] for part in parts)
    rows = sum(sizes)
    width, cols = w_own.shape
    vmem = pl.BlockSpec(memory_space=pltpu.VMEM)
    hbm = pl.BlockSpec(memory_space=pltpu.HBM)
    return pl.pallas_call(
        functools.partial(score_kernel, sizes, width),
        out_shape=jax.ShapeDtypeStruct((rows // 32, LANES), jnp.float32),
        in_specs=[pl.BlockSpec(memory_space=pltpu.SMEM)] + [vmem] * len(parts) + [hbm, hbm],
        out_specs=vmem,
        scratch_shapes=[
            pltpu.VMEM((rows, 2 * cols), jnp.float32),
            pltpu.VMEM((2 * cols // TILE, width, TILE), jnp.bfloat16),
            pltpu.SemaphoreType.DMA((2 * cols // TILE,)),
        ],
        cost_estimate=pl.CostEstimate(
            flops=4 * rows * width * cols, bytes_accessed=4 * width * cols, transcendentals=2 * rows * cols
        ),
        compiler_params=pltpu.CompilerParams(vmem_limit_bytes=22 << 20),
        name="score",
    )(bases, *parts, w_own, w_other)


def table_kernel(place_ref, owner_ref, *refs):
    lines, (out_ref, table) = refs[:-2], refs[-2:]
    table[...] = jnp.zeros_like(table)
    at = 0
    for line in lines:
        for i in range(line.shape[0]):
            table[pl.ds(place_ref[at], 1), :] = line[i : i + 1, :]
            at += 1
    copies = out_ref.shape[0] // table.shape[0]

    def deal(o, carry):
        row = table[pl.ds(owner_ref[o], 1), :]
        for c in range(copies):
            out_ref[pl.ds(o * copies + c, 1), :] = row
        return carry

    lax.fori_loop(0, table.shape[0], deal, 0, unroll=8)


def deal_lines(place, owner, lines, copies):
    smem = pl.BlockSpec(memory_space=pltpu.SMEM)
    vmem = pl.BlockSpec(memory_space=pltpu.VMEM)
    groups = owner.shape[0]
    return pl.pallas_call(
        table_kernel,
        out_shape=jax.ShapeDtypeStruct((groups * copies, LANES), jnp.float32),
        in_specs=[smem, smem] + [vmem] * len(lines),
        out_specs=vmem,
        scratch_shapes=[pltpu.VMEM((groups, LANES), jnp.float32)],
        compiler_params=pltpu.CompilerParams(vmem_limit_bytes=2 << 20),
        name="deal",
    )(place, owner, *lines)


def merge_kernel(length_ref, lines_ref, logprob_ref, entropy_ref):
    lines = lines_ref[...]
    total = pltpu.roll(lines, 96, 1)
    spread = pltpu.roll(lines, 64, 1)
    pick = pltpu.roll(lines, 32, 1)
    lane = lax.broadcasted_iota(jnp.int32, lines.shape, 1)
    live = (total > 0.0) & (lane < 32)
    peak = jnp.max(jnp.where(live, lines, -jnp.inf), axis=0, keepdims=True)
    scale = jnp.where(live, jnp.exp(lines - peak), 0.0)
    exp_total = jnp.sum(jnp.where(live, scale * total, 0.0), axis=0, keepdims=True)
    exp_spread = jnp.sum(jnp.where(live, scale * spread, 0.0), axis=0, keepdims=True)
    picked = jnp.sum(jnp.where(live, pick, 0.0), axis=0, keepdims=True)
    log_total = peak + jnp.log(exp_total)
    keep = lax.broadcasted_iota(jnp.int32, (1, LANES), 1) < length_ref[0]
    slots = logprob_ref.shape[0]
    logprob_ref[...] = jnp.where(keep, picked - log_total, 0.0)[0, :slots]
    entropy_ref[...] = jnp.where(keep, log_total - exp_spread / exp_total, 0.0)[0, :slots]


def merge(lengths, lines, slots):
    vmem = pl.BlockSpec(memory_space=pltpu.VMEM)
    shape = jax.ShapeDtypeStruct((slots,), jnp.float32)
    return pl.pallas_call(
        merge_kernel,
        out_shape=(shape, shape),
        in_specs=[pl.BlockSpec(memory_space=pltpu.SMEM), vmem],
        out_specs=(vmem, vmem),
        compiler_params=pltpu.CompilerParams(vmem_limit_bytes=4 << 20),
        name="merge",
    )(lengths, lines)


PLACES, SPOTS = 32, 4


def guide():
    table = np.zeros((8, 4, 2, 4, PLACES + SPOTS + 2), np.int32)
    steps = {0: ((0, -1), (1, 2), (4, 3), (5, 6)), 1: ((0, -1), (1, -2), (4, 3), (5, 2))}
    hops = [(0, 0), (1, 0), (0, -1), (0, 1), (1, -1), (1, 1), (2, 0), (3, 0)]
    hops += [(2, -1), (2, 1), (3, -1), (3, 1), (0, -2), (1, -2)]
    for z, x, core, tp in np.ndindex(8, 4, 2, 4):
        row = []
        for message, hop in hops + ([(0, 2), (1, 2)] if core == 0 else [(2, 2), (3, 2)]):
            for offset in steps[core][message]:
                if core == 0:
                    at_z = z + hop + (4 if message > 1 else 0)
                    at_x = x + (offset - 4 if message > 1 else offset)
                else:
                    at_z, at_x = z + offset, x + hop
                row.append(((at_z % 8) * 4 + at_x % 4) * 2 + core)
        row += [(tp + k) % 4 for k in (0, 1, 3, 2)]
        row += [((z * 4 + x) * 2 + c) * 4 + tp for c in (core, 1 - core)]
        table[z, x, core, tp] = row
    return jnp.asarray(table.reshape(256, -1))


def local(hidden, gain, head_weight, token_ids, lengths, owner_device):
    slots = hidden.shape[0]
    device = lax.axis_index(ALL)
    index = lax.dynamic_index_in_dim(guide(), device, 0, keepdims=False)
    other_weight = lax.ppermute(head_weight, "core", [(0, 1), (1, 0)])

    ids = token_ids[:, None]
    lane = lax.broadcasted_iota(jnp.int32, (slots, LANES), 1)
    digits = jnp.where(lane == 0, ids >> 12, jnp.where(lane == 1, (ids >> 6) & 63, jnp.where(lane == 2, ids & 63, 0)))
    block = jnp.concatenate([hidden, digits.astype(jnp.bfloat16)], axis=1)
    block, index = lax.optimization_barrier((block, index))
    lines = ring(block, gain, head_weight, other_weight, index)
    dealt = deal_lines(index, owner_device, lines, 4)
    met = lax.all_to_all(dealt, ALL, 0, 0, tiled=True)
    return merge(lengths, met, slots)


def ring(block, gain, head_weight, other_weight, index):
    def move(value, step, swap=False):
        return send(value, step, swap)

    def scored(parts):
        return score(parts, head_weight, other_weight, index)

    def gather(value):
        out = [value]
        for k in (1, 3, 2):
            out.append(lax.ppermute(value, "tp", [(i, (i - k) % 4) for i in range(4)]))
        return out

    first_core = lax.axis_index("core") == 0
    pick = lambda one, two: jnp.where(first_core, one, two)

    around = gather(block)
    far_block = lax.ppermute(block, "zh", [(0, 1), (1, 0)])
    own = norm(index, around, gain)
    own, other_weight = lax.optimization_barrier((own, other_weight))
    head_weight, other_weight = (pltpu.with_memory_space_constraint(w, pltpu.HBM) for w in (head_weight, other_weight))
    f1, b1 = move(own, 1, True), move(own, -1, True)
    beside = gather(far_block)
    partner = norm(index, beside, gain)
    f1p, b1p = move(partner, 1, True), move(partner, -1, True)

    m1 = jnp.concatenate([own, f1], axis=0)
    m1f, m1b = move(m1, 1), move(m1, -1)
    f2 = move(f1, 1, True)
    m2 = jnp.concatenate([b1, f2], axis=0)
    m2f, m2b = move(m2, 1), move(m2, -1)
    m3 = jnp.concatenate([partner, f1p], axis=0)
    m3f, m3b = move(m3, 1), move(m3, -1)
    onward = pick(*lax.optimization_barrier((b1p, b1)))
    b2 = move(onward, -1, True)
    m4 = jnp.concatenate([b1p, b2], axis=0)
    m4f, m4b = move(m4, 1), move(m4, -1)

    c1 = move(jnp.concatenate([m1f, m2f], axis=0), 1)
    x1 = move(pick(m1b, m3b), -1)
    x2 = move(pick(m2b, m4b), -1)
    return [scored([m1, m2, m1f, m1b]), scored([m2f, m2b, m3, m4]), scored([m3f, m3b, m4f, m4b]), scored([c1, x1, x2])]


def solution(mesh):
    split = Mesh(mesh.devices.reshape(SPLIT), ALL)
    placed = (P(REQ, "tp"), P(), P(None, ALL), P(REQ), P(REQ), P())
    return jax.shard_map(local, mesh=split, in_specs=placed, out_specs=(P(REQ), P(REQ)), check_vma=False)
```

```python
import functools

import jax
import jax.numpy as jnp
import numpy as np
from jax import lax
from jax.experimental import pallas as pl
from jax.experimental.pallas import tpu as pltpu
from jax.sharding import Mesh
from jax.sharding import PartitionSpec as P


ALL = ("zh", "zl", "x", "core", "tp")
REQ = ("zh", "zl", "x", "core")
SPLIT = (2, 4, 4, 2, 4)
LANES = 128


def pairs(step, swap):
    out = []
    for z in range(8):
        for x in range(4):
            for core in range(2):
                along_z = (core == 0) != swap
                nz = (z + step) % 8 if along_z else z
                nx = x if along_z else (x + step) % 4
                out.append(((z * 4 + x) * 2 + core, (nz * 4 + nx) * 2 + core))
    return out


def send(value, step, swap):
    return lax.ppermute(value, REQ, pairs(step, swap))


def norm_kernel(eps, spot_ref, *refs):
    pieces, (gain_ref, out_ref) = refs[:-2], refs[-2:]
    quarters = len(pieces)
    width = gain_ref.shape[1] // quarters
    square = jnp.zeros((pieces[0].shape[0], 1), jnp.float32)
    for piece in pieces:
        values = piece[:, :width].astype(jnp.float32)
        square += jnp.sum(values * values, axis=1, keepdims=True)
    scale = lax.rsqrt(square / (width * quarters) + eps)
    for q, piece in enumerate(pieces):
        columns = pl.ds(pl.multiple_of(spot_ref[PLACES + q] * width, LANES), width)
        values = piece[:, :width].astype(jnp.float32)
        out_ref[:, columns] = (values * scale * gain_ref[:, columns]).astype(jnp.bfloat16)
    out_ref[:, quarters * width :] = pieces[0][:, width:]


def norm(spots, pieces, gain):
    vmem = pl.BlockSpec(memory_space=pltpu.VMEM)
    return pl.pallas_call(
        functools.partial(norm_kernel, 1e-05),
        out_shape=jax.ShapeDtypeStruct((pieces[0].shape[0], gain.shape[0] + LANES), jnp.bfloat16),
        in_specs=[pl.BlockSpec(memory_space=pltpu.SMEM)] + [vmem] * (len(pieces) + 1),
        out_specs=vmem,
        compiler_params=pltpu.CompilerParams(vmem_limit_bytes=4 << 20),
        name="norm",
    )(spots, *pieces, gain[None, :])


TILE = 256


def score_kernel(sizes, width, base_ref, *refs):
    n = len(sizes)
    parts, (w_own, w_other, out_ref, logits) = refs[:n], refs[n:]
    cols = w_own.shape[1]
    for half, w in enumerate((w_own, w_other)):

        def column_tile(i, carry, half=half, w=w):
            lhs = jnp.concatenate([part[:, :width] for part in parts], axis=0)
            product = jnp.dot(lhs, w[:, pl.ds(pl.multiple_of(i * TILE, TILE), TILE)], preferred_element_type=jnp.float32)
            logits[:, pl.ds(pl.multiple_of(half * cols + i * TILE, TILE), TILE)] = product
            return carry

        lax.fori_loop(0, cols // TILE, column_tile, 0)

    lane = lax.broadcasted_iota(jnp.int32, (32, LANES), 1)
    slot = lax.broadcasted_iota(jnp.int32, (32, LANES), 0)
    column = lax.broadcasted_iota(jnp.int32, (32, 2 * cols), 1)
    first_base, second_base = (base_ref[PLACES + SPOTS + i] * cols for i in range(2))
    vocab = jnp.where(column < cols, first_base + column, second_base + column - cols)
    digit = jnp.where(lane == 0, 4096.0, jnp.where(lane == 1, 64.0, jnp.where(lane == 2, 1.0, 0.0)))
    before = 0
    for part, rows in zip(parts, sizes):

        def group(g, carry, part=part, before=before):
            row = pl.multiple_of(g * 32, 32)
            lg = logits[pl.ds(pl.multiple_of(before + g * 32, 32), 32), :]
            code = part[pl.ds(row, 32), pl.ds(width, LANES)].astype(jnp.float32)
            ids = jnp.sum(code * digit, axis=1, keepdims=True).astype(jnp.int32)
            peak = jnp.max(lg, axis=1, keepdims=True)
            weight = jnp.exp(lg - peak)
            total = jnp.sum(weight, axis=1, keepdims=True)
            spread = jnp.sum(weight * lg, axis=1, keepdims=True)
            pick = jnp.sum(jnp.where(vocab == ids, lg, 0.0), axis=1, keepdims=True)
            stat = jnp.where(lane < 32, peak, jnp.where(lane < 64, total, jnp.where(lane < 96, spread, pick)))
            line = jnp.sum(jnp.where(lane % 32 == slot, stat, 0.0), axis=0, keepdims=True)
            out_ref[pl.ds(before // 32 + g, 1), :] = line
            return carry

        lax.fori_loop(0, rows // 32, group, 0)
        before += rows


def score(parts, w_own, w_other, bases):
    sizes = tuple(part.shape[0] for part in parts)
    rows = sum(sizes)
    width, cols = w_own.shape
    vmem = pl.BlockSpec(memory_space=pltpu.VMEM)
    return pl.pallas_call(
        functools.partial(score_kernel, sizes, width),
        out_shape=jax.ShapeDtypeStruct((rows // 32, LANES), jnp.float32),
        in_specs=[pl.BlockSpec(memory_space=pltpu.SMEM)] + [vmem] * (len(parts) + 2),
        out_specs=vmem,
        scratch_shapes=[pltpu.VMEM((rows, 2 * cols), jnp.float32)],
        cost_estimate=pl.CostEstimate(
            flops=4 * rows * width * cols, bytes_accessed=4 * width * cols, transcendentals=2 * rows * cols
        ),
        compiler_params=pltpu.CompilerParams(vmem_limit_bytes=16 << 20),
        name="score",
    )(bases, *parts, w_own, w_other)


def table_kernel(place_ref, owner_ref, *refs):
    lines, (out_ref, table) = refs[:-2], refs[-2:]
    table[...] = jnp.zeros_like(table)
    at = 0
    for line in lines:
        for i in range(line.shape[0]):
            table[pl.ds(place_ref[at], 1), :] = line[i : i + 1, :]
            at += 1
    copies = out_ref.shape[0] // table.shape[0]

    def deal(o, carry):
        row = table[pl.ds(owner_ref[o], 1), :]
        for c in range(copies):
            out_ref[pl.ds(o * copies + c, 1), :] = row
        return carry

    lax.fori_loop(0, table.shape[0], deal, 0, unroll=8)


def deal_lines(place, owner, lines, copies):
    smem = pl.BlockSpec(memory_space=pltpu.SMEM)
    vmem = pl.BlockSpec(memory_space=pltpu.VMEM)
    groups = owner.shape[0]
    return pl.pallas_call(
        table_kernel,
        out_shape=jax.ShapeDtypeStruct((groups * copies, LANES), jnp.float32),
        in_specs=[smem, smem] + [vmem] * len(lines),
        out_specs=vmem,
        scratch_shapes=[pltpu.VMEM((groups, LANES), jnp.float32)],
        compiler_params=pltpu.CompilerParams(vmem_limit_bytes=2 << 20),
        name="deal",
    )(place, owner, *lines)


def merge_kernel(length_ref, lines_ref, logprob_ref, entropy_ref):
    lines = lines_ref[...]
    total = pltpu.roll(lines, 96, 1)
    spread = pltpu.roll(lines, 64, 1)
    pick = pltpu.roll(lines, 32, 1)
    lane = lax.broadcasted_iota(jnp.int32, lines.shape, 1)
    live = (total > 0.0) & (lane < 32)
    peak = jnp.max(jnp.where(live, lines, -jnp.inf), axis=0, keepdims=True)
    scale = jnp.where(live, jnp.exp(lines - peak), 0.0)
    exp_total = jnp.sum(jnp.where(live, scale * total, 0.0), axis=0, keepdims=True)
    exp_spread = jnp.sum(jnp.where(live, scale * spread, 0.0), axis=0, keepdims=True)
    picked = jnp.sum(jnp.where(live, pick, 0.0), axis=0, keepdims=True)
    log_total = peak + jnp.log(exp_total)
    keep = lax.broadcasted_iota(jnp.int32, (1, LANES), 1) < length_ref[0]
    slots = logprob_ref.shape[0]
    logprob_ref[...] = jnp.where(keep, picked - log_total, 0.0)[0, :slots]
    entropy_ref[...] = jnp.where(keep, log_total - exp_spread / exp_total, 0.0)[0, :slots]


def merge(lengths, lines, slots):
    vmem = pl.BlockSpec(memory_space=pltpu.VMEM)
    shape = jax.ShapeDtypeStruct((slots,), jnp.float32)
    return pl.pallas_call(
        merge_kernel,
        out_shape=(shape, shape),
        in_specs=[pl.BlockSpec(memory_space=pltpu.SMEM), vmem],
        out_specs=(vmem, vmem),
        compiler_params=pltpu.CompilerParams(vmem_limit_bytes=4 << 20),
        name="merge",
    )(lengths, lines)


PLACES, SPOTS = 32, 4


def guide():
    table = np.zeros((8, 4, 2, 4, PLACES + SPOTS + 2), np.int32)
    steps = {0: ((0, -1), (1, 2), (4, 3), (5, 6)), 1: ((0, -1), (1, -2), (4, 3), (5, 2))}
    hops = [(0, 0), (1, 0), (0, -1), (0, 1), (1, -1), (1, 1), (2, 0), (3, 0)]
    hops += [(2, -1), (2, 1), (3, -1), (3, 1), (0, -2), (1, -2)]
    for z, x, core, tp in np.ndindex(8, 4, 2, 4):
        row = []
        for message, hop in hops + ([(0, 2), (1, 2)] if core == 0 else [(2, 2), (3, 2)]):
            for offset in steps[core][message]:
                if core == 0:
                    at_z = z + hop + (4 if message > 1 else 0)
                    at_x = x + (offset - 4 if message > 1 else offset)
                else:
                    at_z, at_x = z + offset, x + hop
                row.append(((at_z % 8) * 4 + at_x % 4) * 2 + core)
        row += [(tp + k) % 4 for k in (0, 1, 3, 2)]
        row += [((z * 4 + x) * 2 + c) * 4 + tp for c in (core, 1 - core)]
        table[z, x, core, tp] = row
    return jnp.asarray(table.reshape(256, -1))


def local(hidden, gain, head_weight, token_ids, lengths, owner_device):
    slots = hidden.shape[0]
    device = lax.axis_index(ALL)
    index = lax.dynamic_index_in_dim(guide(), device, 0, keepdims=False)
    other_weight = lax.ppermute(head_weight, "core", [(0, 1), (1, 0)])

    ids = token_ids[:, None]
    lane = lax.broadcasted_iota(jnp.int32, (slots, LANES), 1)
    digits = jnp.where(lane == 0, ids >> 12, jnp.where(lane == 1, (ids >> 6) & 63, jnp.where(lane == 2, ids & 63, 0)))
    block = jnp.concatenate([hidden, digits.astype(jnp.bfloat16)], axis=1)
    block, index = lax.optimization_barrier((block, index))
    lines = ring(block, gain, head_weight, other_weight, index)
    dealt = deal_lines(index, owner_device, lines, 4)
    met = lax.all_to_all(dealt, ALL, 0, 0, tiled=True)
    return merge(lengths, met, slots)


def ring(block, gain, head_weight, other_weight, index):
    def move(value, step, swap=False):
        return send(value, step, swap)

    def scored(parts):
        return score(parts, head_weight, other_weight, index)

    def gather(value):
        out = [value]
        for k in (1, 3, 2):
            out.append(lax.ppermute(value, "tp", [(i, (i - k) % 4) for i in range(4)]))
        return out

    first_core = lax.axis_index("core") == 0
    pick = lambda one, two: jnp.where(first_core, one, two)

    around = gather(block)
    far_block = lax.ppermute(block, "zh", [(0, 1), (1, 0)])
    own = norm(index, around, gain)
    own, other_weight = lax.optimization_barrier((own, other_weight))
    f1, b1 = move(own, 1, True), move(own, -1, True)
    beside = gather(far_block)
    partner = norm(index, beside, gain)
    f1p, b1p = move(partner, 1, True), move(partner, -1, True)

    m1 = jnp.concatenate([own, f1], axis=0)
    m1f, m1b = move(m1, 1), move(m1, -1)
    f2 = move(f1, 1, True)
    m2 = jnp.concatenate([b1, f2], axis=0)
    m2f, m2b = move(m2, 1), move(m2, -1)
    m3 = jnp.concatenate([partner, f1p], axis=0)
    m3f, m3b = move(m3, 1), move(m3, -1)
    onward = pick(*lax.optimization_barrier((b1p, b1)))
    b2 = move(onward, -1, True)
    m4 = jnp.concatenate([b1p, b2], axis=0)
    m4f, m4b = move(m4, 1), move(m4, -1)

    c1 = move(jnp.concatenate([m1f, m2f], axis=0), 1)
    x1 = move(pick(m1b, m3b), -1)
    x2 = move(pick(m2b, m4b), -1)
    return [scored([m1, m2, m1f, m1b]), scored([m2f, m2b, m3, m4]), scored([m3f, m3b, m4f, m4b]), scored([c1, x1, x2])]


def solution(mesh):
    split = Mesh(mesh.devices.reshape(SPLIT), ALL)
    placed = (P(REQ, "tp"), P(), P(None, ALL), P(REQ), P(REQ), P())
    return jax.shard_map(local, mesh=split, in_specs=placed, out_specs=(P(REQ), P(REQ)), check_vma=False)
```
